128 devices in a mesh: blk: 32 (over y, x, z_lo), grp: 4 (over z_hi, core).
Axes of the slice: x: 4, y: 4, z: 4 (z_hi: 2, z_lo: 2; z = z_hi * 2 + z_lo), core: 2. Of those that a mesh axis runs over, the one named last changes fastest.
Arguments:
- queries: float32 [16384, 1024], P(('blk', 'grp')), may hold values from -48 to 48
- passages: float32 [16384, 1024], P(('blk', 'grp')), may hold values from -48 to 48
- hard_table: bfloat16 [98304, 1024], P(('blk', 'grp')), may hold values from -12 to 12
- hard_index: int32 [16384, 8], P(('blk', 'grp')), may hold values from 0 to 3071, as said below
Outputs:
- mean_loss: float32 [], replicated
- query_grad: float32 [16384, 1024], P(('blk', 'grp'))
- passage_grad: float32 [16384, 1024], P(('blk', 'grp'))
- table_grad: bfloat16 [98304, 1024], P(('blk', 'grp'))
The draws below stay inside these ranges and needn't reach their ends.
Inputs may be any that keep to these rules, and one draw needn't show every extreme that they name: Owner o = hard_index // 768 is a batch group of the query's own loop shard. Among the 1024 entries of one device, the four owners are named exactly 384, 256, 256 and 128 times in some order, and the owner named 3 * 128 times is the same for all devices of one loop shard; entries may repeat.
All inputs are finite; a program needn't handle non-finite values.
Results may differ from the reference program's by a relative error of at most 0.0038.
Values may be sent and summed in bfloat16 or wider, within the bound.
No kernel may reach another device: no remote copies, remote signals or barrier semaphores. Data moves between devices by JAX's collectives and lax.ppermute only.
A program may use at most 64 MiB of HBM per device.

```python
import math
import jax
import jax.numpy as jnp
from jax import lax

D = 1024
ROWS = 128
STOPS = 4
HARD = 8
HARD_DEV = 768
GROUPS = 4
BLOCKS = 32
BATCH = 16384
HARD_ROWS = 98304


def shared_pairs(key):
    base_key = jax.random.fold_in(key, 11)
    key_u, key_p, key_q, key_n = jax.random.split(base_key, 4)
    block_shape = (BLOCKS, GROUPS, ROWS, D)
    fresh = jnp.clip(jax.random.normal(key_u, block_shape, jnp.float32), -6.0, 6.0)
    noise_one = jnp.clip(jax.random.normal(key_n, (BATCH, D), jnp.float32), -6.0, 6.0)
    mixed = fresh + jnp.roll(fresh, -1, axis=0)
    mixed = mixed + jnp.roll(fresh, -2, axis=0)
    mixed = mixed + jnp.roll(fresh, -3, axis=0)
    direction = (0.5 * mixed).reshape(BATCH, D)
    own_dir = fresh.reshape(BATCH, D)
    device_total = BATCH // ROWS
    device_pos = (jnp.arange(BATCH) // ROWS).astype(jnp.float32) / (device_total - 1.0)
    align = (0.95 - 0.8 * device_pos)[:, None]
    spread = jnp.sqrt(1.0 - align * align)
    row_scale = jnp.exp(jax.random.uniform(key_p, (GROUPS, ROWS), jnp.float32, math.log(0.5), math.log(5.0)))
    pass_scale = jnp.broadcast_to(row_scale[None], (BLOCKS, GROUPS, ROWS)).reshape(BATCH, 1)
    level = jnp.exp(jax.random.uniform(key_q, (BATCH, 1), jnp.float32, math.log(0.8), math.log(1.6)))
    query_scale = level / pass_scale
    passage_vals = pass_scale * direction
    query_vals = query_scale * (align * own_dir + spread * noise_one)
    return (jnp.clip(query_vals, -48.0, 48.0), jnp.clip(passage_vals, -48.0, 48.0))


def draw_queries(key, part):
    return shared_pairs(key)[0]


def draw_passages(key, part):
    return shared_pairs(key)[1]


def draw_hard_index(key, part):
    device_count = BATCH // ROWS
    shard_count = device_count // GROUPS
    slot_keys = jax.random.split(jax.random.fold_in(key, 21), device_count)
    orders = jax.vmap(lambda each_key: jax.random.permutation(each_key, HARD * ROWS))(slot_keys)
    class_table = jnp.concatenate([jnp.zeros((3 * ROWS,), jnp.int32), jnp.ones((2 * ROWS,), jnp.int32), jnp.full((2 * ROWS,), 2, jnp.int32), jnp.full((ROWS,), 3, jnp.int32)])
    classes = class_table[orders]
    owner_keys = jax.random.split(jax.random.fold_in(key, 22), shard_count)
    owner_perm = jax.vmap(lambda each_key: jax.random.permutation(each_key, GROUPS))(owner_keys)
    shard_of_device = (jnp.arange(device_count) // GROUPS).astype(jnp.int32)
    device_perm = owner_perm[shard_of_device]
    owner_ids = jnp.take_along_axis(device_perm, classes, axis=1)
    row_ids = jax.random.randint(jax.random.fold_in(key, 23), (BATCH, HARD), 0, HARD_DEV, jnp.int32)
    return (owner_ids.reshape(BATCH, HARD) * HARD_DEV + row_ids).astype(jnp.int32)


def level_of(key, dims, pieces, least, largest):
    gain, own = 1.0, jax.random.fold_in(key, 6)
    for dim, parts in pieces:
        steps = jnp.exp(jax.random.uniform(jax.random.fold_in(own, dim), (parts,), jnp.float32, least / len(pieces), largest / len(pieces)))
        gain = gain * jnp.repeat(steps, dims[dim] // parts).reshape([-1 if axis == dim else 1 for axis in range(len(dims))])
    return gain


def normal_values(stream_key, shape, scale, most, cuts=(), kind=jnp.bfloat16):
    result = jax.random.normal(stream_key, shape, jnp.float32) * scale
    if len(cuts) > 0:
        result = level_of(stream_key, shape, cuts, -0.22, 0.18) * result
    return jnp.clip(result, min=-most, max=most).astype(kind)


def setup_inputs(seed: int = 0) -> dict:
    seeds = jax.random.split(jax.random.key(seed), 5)
    queries = draw_queries(jax.random.fold_in(seeds[4], 71), 0)
    passages = draw_passages(jax.random.fold_in(seeds[4], 71), 0)
    hard_table = normal_values(seeds[2], (HARD_ROWS, D), 2.0, 12.0, ((0, 128),))
    hard_index = draw_hard_index(jax.random.fold_in(seeds[4], 71), 0)
    return dict(queries=queries, passages=passages, hard_table=hard_table, hard_index=hard_index)


score_scale = 0.015625


def reference(queries, passages, hard_table, hard_index):
    query_split = queries.reshape(BLOCKS, GROUPS, ROWS, D)
    passage_split = passages.reshape(BLOCKS, GROUPS, ROWS, D)
    table_split = hard_table.reshape(BLOCKS, GROUPS * HARD_DEV, D)
    index_split = hard_index.reshape(BLOCKS, GROUPS, ROWS, HARD)
    highest = lax.Precision.HIGHEST

    def per_shard(shard):
        query_blk = query_split[shard]
        own_pass = passage_split[shard]
        window = jnp.stack([passage_split[(shard - stop_index) % BLOCKS] for stop_index in range(STOPS)])
        win_scores = jnp.einsum('grd,sgjd->grsj', query_blk, window, precision=highest) * score_scale
        hard_vecs = table_split[shard][index_split[shard]].astype(jnp.float32)
        hard_scores = jnp.einsum('grd,grkd->grk', query_blk, hard_vecs, precision=highest) * score_scale
        positive = jnp.sum(query_blk * own_pass, axis=-1) * score_scale
        joined = jnp.concatenate([win_scores.reshape(GROUPS, ROWS, STOPS * ROWS), hard_scores], axis=-1)
        top_val = jnp.max(joined, axis=-1)
        lse = top_val + jnp.log(jnp.sum(jnp.exp(joined - top_val[..., None]), axis=-1))
        loss_part = jnp.sum(lse - positive)
        weight = jnp.exp(win_scores - lse[:, :, None, None])
        hard_weight = jnp.exp(hard_scores - lse[..., None])
        grad_query = score_scale * (jnp.einsum('grsj,sgjd->grd', weight, window, precision=highest)
                                    + jnp.einsum('grk,grkd->grd', hard_weight, hard_vecs, precision=highest)
                                    - own_pass)
        grad_window = score_scale * jnp.einsum('grsj,grd->sgjd', weight, query_blk, precision=highest)
        grad_window = grad_window.at[0].add(-score_scale * query_blk)
        hard_term = (score_scale * hard_weight[..., None] * query_blk[:, :, None, :]).astype(jnp.bfloat16)
        hard_term = lax.optimization_barrier(hard_term).astype(jnp.float32)
        table_part = jnp.zeros((GROUPS * HARD_DEV, D), jnp.float32)
        table_part = table_part.at[index_split[shard].reshape(-1)].add(hard_term.reshape(-1, D))
        return loss_part, grad_query, grad_window, table_part

    loss_parts, grad_query, grad_window, table_parts = lax.map(per_shard, jnp.arange(BLOCKS, dtype=jnp.int32))
    grad_pass = jnp.zeros((BLOCKS, GROUPS, ROWS, D), jnp.float32)
    for stop_index in range(STOPS):
        grad_pass = grad_pass + jnp.roll(grad_window[:, stop_index], -stop_index, axis=0)
    mean_loss = jnp.sum(loss_parts) / BATCH
    return (mean_loss, grad_query.reshape(BATCH, D), grad_pass.reshape(BATCH, D),
            table_parts.reshape(HARD_ROWS, D).astype(jnp.bfloat16))
```

```python
import jax
import jax.numpy as jnp
from jax import lax
from jax.experimental import pallas as pl
from jax.experimental.pallas import tpu as pltpu
from jax.sharding import Mesh
from jax.sharding import PartitionSpec as P

STOPS = 4
GRP = ("grp_0", "grp_1")
BLK = ("blk_0", "blk_1", "blk_2")
BLK_GRP = ("blk_0", "blk_1", "blk_2", "grp_0", "grp_1")

score_scale = 0.015625
FLOOR = -1.0e30
F32 = jnp.float32
BF16 = jnp.bfloat16


def along_loop(value, by, only=None):
    length = lax.axis_size(BLK)
    pairs = [(i, (i + by) % length) for i in range(length) if only is None or i % 2 == only]
    return lax.ppermute(value, BLK, pairs)


def swapped(value, axis):
    return lax.ppermute(value, axis, [(0, 1), (1, 0)])


def crossed(value):
    return lax.ppermute(value, GRP, [(0, 3), (1, 2), (2, 1), (3, 0)])


def mm(a, b, ca, cb):
    return lax.dot_general(a, b, (((ca,), (cb,)), ((), ())), preferred_element_type=F32)


def exact_mm(a, b, ca, cb):
    return lax.dot_general(
        a, b, (((ca,), (cb,)), ((), ())), precision=lax.Precision.HIGHEST, preferred_element_type=F32
    )


def split2(x):
    hi = x.astype(BF16)
    return hi, (x - hi.astype(F32)).astype(BF16)


def split3(x):
    hi = x.astype(BF16)
    rest = x - hi.astype(F32)
    mid = rest.astype(BF16)
    return hi, mid, (rest - mid.astype(F32)).astype(BF16)


def mm3(a, b, ca, cb):
    a_hi, a_lo = split2(a)
    b_hi, b_lo = split2(b)
    return mm(a_hi, b_hi, ca, cb) + (mm(a_hi, b_lo, ca, cb) + mm(a_lo, b_hi, ca, cb))


def table_scores(table, query_stack, index_rows, base, width):
    wide = mm(table, query_stack, 1, 1)
    score = (wide[:, :width] + (wide[:, width : 2 * width] + wide[:, 2 * width :])) * score_scale
    row_id = lax.broadcasted_iota(jnp.int32, score.shape, 0) + base
    count = jnp.zeros(score.shape, F32)
    for k in range(index_rows.shape[0]):
        count = count + jnp.where(index_rows[k : k + 1, :] == row_id, 1.0, 0.0)
    return jnp.where(count > 0.0, score + jnp.log(jnp.maximum(count, 1.0)), FLOOR)


def hard_kernel(base_ref, query_ref, index_ref, own_ref, other_ref, named_ref, sum_ref, stat_ref):
    width = query_ref.shape[0]
    query_stack = jnp.concatenate(split3(query_ref[...]), axis=0)
    index_rows = index_ref[...]
    first = table_scores(own_ref[...], query_stack, index_rows, base_ref[0], width)
    second = table_scores(other_ref[...], query_stack, index_rows, base_ref[1], width)
    named_ref[...] = first
    top = jnp.maximum(jnp.max(first, axis=0, keepdims=True), jnp.max(second, axis=0, keepdims=True))
    first = jnp.exp(first - top)
    second = jnp.exp(second - top)
    total = jnp.sum(first, axis=0, keepdims=True) + jnp.sum(second, axis=0, keepdims=True)
    pair = mm(jnp.concatenate(split2(first), axis=1), own_ref[...], 0, 0)
    pair = pair + mm(jnp.concatenate(split2(second), axis=1), other_ref[...], 0, 0)
    sum_ref[...] = pair[:width] + pair[width:]
    stat_ref[...] = jnp.concatenate(
        [jnp.broadcast_to(top, (4, width)), jnp.broadcast_to(total, (4, width))], axis=0
    )


def named_kernel(base_ref, query_ref, index_ref, own_ref, named_ref):
    width = query_ref.shape[0]
    query_stack = jnp.concatenate(split3(query_ref[...]), axis=0)
    named_ref[...] = table_scores(own_ref[...], query_stack, index_ref[...], base_ref[0], width)


def window_kernel(
    even_ref, query_ref, p0_ref, p1e_ref, p1o_ref, p2_ref, p3_ref, stat_ref, far_ref, score_ref, lse_ref, loss_ref
):
    rows = query_ref.shape[0]
    query = query_ref[...]
    p1 = jnp.where(even_ref[0] == 1, p1e_ref[...], p1o_ref[...])
    scores = []
    for stop, block in enumerate((p0_ref[...], p1, p2_ref[...], p3_ref[...])):
        score = exact_mm(block, query, 1, 1) * score_scale
        score_ref[stop * rows : (stop + 1) * rows, :] = score
        scores.append(score)
    eye = lax.broadcasted_iota(jnp.int32, (rows, rows), 0) == lax.broadcasted_iota(jnp.int32, (rows, rows), 1)
    positive = jnp.sum(jnp.where(eye, scores[0], 0.0), axis=0, keepdims=True)
    stat, far = stat_ref[...], far_ref[...]
    top = jnp.maximum(stat[0:1], far[0:1])
    for score in scores:
        top = jnp.maximum(top, jnp.max(score, axis=0, keepdims=True))
    total = stat[4:5] * jnp.exp(stat[0:1] - top) + far[4:5] * jnp.exp(far[0:1] - top)
    for score in scores:
        total = total + jnp.sum(jnp.exp(score - top), axis=0, keepdims=True)
    lse = top + jnp.log(total)
    lse_ref[...] = jnp.broadcast_to(lse, lse_ref.shape)
    loss_ref[...] = jnp.broadcast_to(lse - positive, loss_ref.shape)


def query_grad_kernel(
    even_ref, score_ref, lse_ref, p0_ref, p1e_ref, p1o_ref, p2_ref, p3_ref, stat_ref, near_ref, farstat_ref, far_ref, out_ref
):
    rows = p0_ref.shape[0]
    lse = lse_ref[0:1, :]
    p1 = jnp.where(even_ref[0] == 1, p1e_ref[...], p1o_ref[...])
    eye = lax.broadcasted_iota(jnp.int32, (rows, rows), 0) == lax.broadcasted_iota(jnp.int32, (rows, rows), 1)

    def column(row):
        return jnp.sum(jnp.where(eye, jnp.broadcast_to(row, (rows, rows)), 0.0), axis=1, keepdims=True)

    total = column(jnp.exp(stat_ref[0:1, :] - lse)) * near_ref[...]
    total = total + column(jnp.exp(farstat_ref[0:1, :] - lse)) * far_ref[...]
    for stop, block in enumerate((p0_ref[...], p1, p2_ref[...], p3_ref[...])):
        weight = jnp.exp(score_ref[stop * rows : (stop + 1) * rows, :] - lse)
        total = total + mm3(weight, block, 0, 0)
    out_ref[...] = score_scale * (total - p0_ref[...])


def back_score_kernel(even_ref, p_ref, q2_ref, qx_ref, qe_ref, qo_ref, score_ref, pick_ref):
    rows = p_ref.shape[0]
    passage = p_ref[...]
    pick = jnp.where(even_ref[0] == 1, qe_ref[...], qo_ref[...])
    pick_ref[...] = pick
    for slot, block in enumerate((q2_ref[...], qx_ref[...], pick)):
        score_ref[:, slot * rows : (slot + 1) * rows] = exact_mm(passage, block, 1, 1) * score_scale


def passage_grad_kernel(
    even_ref, own_score_ref, score_ref, q0_ref, q2_ref, qx_ref, pick_ref, l0_ref, l1_ref, l2_ref, l3_ref, out_ref
):
    rows = q0_ref.shape[0]
    even = even_ref[0] == 1
    l1, l3 = l1_ref[0:1, :], l3_ref[0:1, :]
    lx = jnp.where(even, l3, l1)
    lp = jnp.where(even, l1, l3)
    total = mm3(jnp.exp(own_score_ref[:rows, :] - l0_ref[0:1, :]), q0_ref[...], 1, 0)
    for slot, (block, lse) in enumerate(((q2_ref[...], l2_ref[0:1, :]), (qx_ref[...], lx), (pick_ref[...], lp))):
        weight = jnp.exp(score_ref[:, slot * rows : (slot + 1) * rows] - lse)
        total = total + mm3(weight, block, 1, 0)
    out_ref[...] = score_scale * total - score_scale * q0_ref[...]


def table_grad_kernel(
    n0_ref, n1_ref, n23_ref, q0_ref, q1_ref, q23_ref, l0_ref, l1_ref, l2_ref, l3_ref, out_ref
):
    rows = q0_ref.shape[0]
    total = mm3(jnp.exp(n0_ref[...] - l0_ref[0:1, :]), q0_ref[...], 1, 0)
    total = total + mm3(jnp.exp(n1_ref[...] - l1_ref[0:1, :]), q1_ref[...], 1, 0)
    lse = jnp.concatenate([l2_ref[0:1, :], l3_ref[0:1, :]], axis=1)
    total = total + mm3(jnp.exp(n23_ref[...] - lse), q23_ref[...], 1, 0)
    out_ref[...] = (score_scale * total).astype(out_ref.dtype)


SMEM = pl.BlockSpec(memory_space=pltpu.SMEM)
VMEM = pl.BlockSpec(memory_space=pltpu.VMEM)


def call(kernel, name, outs, *args, scalars=0):
    return pl.pallas_call(
        kernel,
        name=name,
        out_shape=[jax.ShapeDtypeStruct(s, d) for s, d in outs],
        in_specs=[SMEM] * scalars + [VMEM] * (len(args) - scalars),
        out_specs=[VMEM] * len(outs),
        compiler_params=pltpu.CompilerParams(vmem_limit_bytes=48 * 1024 * 1024),
    )(*args)


def local(queries, passages, hard_table, hard_index):
    rows, width = queries.shape
    table_rows = hard_table.shape[0]
    device_count = lax.axis_size(BLK) * lax.axis_size(GRP)
    index = hard_index.T
    even = (1 - lax.axis_index("blk_2")).astype(jnp.int32).reshape(1)
    mine = lax.axis_index(GRP).astype(jnp.int32)
    base = jnp.stack([mine, mine ^ 1]) * table_rows

    p_two = along_loop(passages, 2)
    p_side = swapped(passages, "blk_2")
    other_table = swapped(hard_table, "grp_1")
    q_far = swapped(queries, "grp_0")
    i_far = swapped(index, "grp_0")
    q_two = along_loop(queries, -2)
    p_one = along_loop(p_side, 2, only=0)
    p_three = along_loop(p_two, 1)
    q_side = swapped(queries, "blk_2")
    q_pair = swapped(jnp.concatenate([queries, q_far], axis=0), "grp_1")
    i_pair = swapped(jnp.concatenate([index, i_far], axis=1), "grp_1")

    hard_out = [((table_rows, rows), F32), ((rows, width), F32), ((8, rows), F32)]
    named_0, near_sum, near_stat = call(
        hard_kernel, "hard", hard_out, base, queries, index, hard_table, other_table, scalars=1
    )
    named_1, far_made, far_made_stat = call(
        hard_kernel, "hard", hard_out, base, q_far, i_far, hard_table, other_table, scalars=1
    )
    far_stat = swapped(far_made_stat, "grp_0")
    far_sum = swapped(far_made, "grp_0")
    (named_23,) = call(
        named_kernel, "named", [((table_rows, 2 * rows), F32)], base, q_pair, i_pair, hard_table, scalars=1
    )
    q_cross = along_loop(q_side, -2)
    q_last = along_loop(q_cross, -2, only=1)

    score, lse, loss = call(
        window_kernel,
        "window",
        [((STOPS * rows, rows), F32), ((8, rows), F32), ((device_count, rows), F32)],
        even, queries, passages, p_one, p_side, p_two, p_three, near_stat, far_stat,
        scalars=1,
    )
    lse_far = swapped(lse, "grp_0")
    lse_near = swapped(lse, "grp_1")
    lse_cross = crossed(lse)
    lse_1 = along_loop(lse, -1)
    lse_2 = along_loop(lse, -2)
    lse_3 = along_loop(lse, -3)
    losses = lax.all_to_all(loss, BLK_GRP, 0, 0, tiled=True)
    mean_loss = jnp.sum(losses) / (rows * device_count)

    (query_grad,) = call(
        query_grad_kernel, "query_grad", [((rows, width), F32)],
        even, score, lse, passages, p_one, p_side, p_two, p_three, near_stat, near_sum, far_stat, far_sum,
        scalars=1,
    )
    back_score, q_pick = call(
        back_score_kernel, "back_score", [((rows, 3 * rows), F32), ((rows, width), F32)],
        even, passages, q_two, q_cross, q_side, q_last,
        scalars=1,
    )
    (passage_grad,) = call(
        passage_grad_kernel, "passage_grad", [((rows, width), F32)],
        even, score, back_score, queries, q_two, q_cross, q_pick, lse, lse_1, lse_2, lse_3,
        scalars=1,
    )
    (table_grad,) = call(
        table_grad_kernel, "table_grad", [((table_rows, width), BF16)],
        named_0, named_1, named_23, queries, q_far, q_pair, lse, lse_far, lse_near, lse_cross,
    )
    return (mean_loss, query_grad, passage_grad, table_grad)


def solution(mesh):
    finer = Mesh(mesh.devices.reshape(4, 4, 2, 2, 2), ("blk_0", "blk_1", "blk_2", "grp_0", "grp_1"))
    in_specs = (P(BLK_GRP, None), P(BLK_GRP, None), P(BLK_GRP, None), P(BLK_GRP, None))
    out_specs = (P(), P(BLK_GRP, None), P(BLK_GRP, None), P(BLK_GRP, None))
    return jax.shard_map(local, mesh=finer, in_specs=in_specs, out_specs=out_specs, check_vma=False)
```

```python
import jax
import jax.numpy as jnp
from jax import lax
from jax.experimental import pallas as pl
from jax.experimental.pallas import tpu as pltpu
from jax.sharding import Mesh
from jax.sharding import PartitionSpec as P


GRP = ("grp_0", "grp_1")
BLK = ("blk_0", "blk_1", "blk_2")
BLK_GRP = ("blk_0", "blk_1", "blk_2", "grp_0", "grp_1")

score_scale = 0.015625
FLOOR = -1.0e30
TABLE_BLOCK = 256
F32 = jnp.float32
BF16 = jnp.bfloat16


def along_loop(value, by):
    length = lax.axis_size(BLK)
    return lax.ppermute(value, BLK, [(i, (i + by) % length) for i in range(length)])


def swapped(value, axis):
    return lax.ppermute(value, axis, [(0, 1), (1, 0)])


def crossed(value):
    return lax.ppermute(value, GRP, [(0, 3), (1, 2), (2, 1), (3, 0)])


def mm(a, b, ca, cb):
    return lax.dot_general(a, b, (((ca,), (cb,)), ((), ())), preferred_element_type=F32)


def split2(x):
    hi = x.astype(BF16)
    return hi, (x - hi.astype(F32)).astype(BF16)


def split3(x):
    hi = x.astype(BF16)
    rest = x - hi.astype(F32)
    mid = rest.astype(BF16)
    return hi, mid, (rest - mid.astype(F32)).astype(BF16)


def table_scores(wide, index_rows, base):
    width = wide.shape[1] // 3
    score = (wide[:, :width] + (wide[:, width : 2 * width] + wide[:, 2 * width :])) * score_scale
    row_id = lax.broadcasted_iota(jnp.int32, score.shape, 0) + base
    count = jnp.zeros(score.shape, F32)
    for k in range(index_rows.shape[0]):
        count = count + jnp.where(index_rows[k : k + 1, :] == row_id, 1.0, 0.0)
    return jnp.where(count > 0.0, score + jnp.log(jnp.maximum(count, 1.0)), FLOOR)


class Source:
    def __init__(self, ref, copy=None):
        self.ref, self.copy = ref, copy

    def get(self):
        if self.copy is not None:
            self.copy.wait()
            self.copy = None
        return self.ref[...]


class Sink:
    def __init__(self, target, ref, sem):
        self.target, self.ref, self.sem, self.copies = target, ref, sem, []

    def start(self, target, ref):
        copy = pltpu.make_async_copy(ref, target, self.sem.at[len(self.copies)])
        copy.start()
        self.copies.append(copy)

    def put(self, value):
        self.ref[...] = value.astype(self.ref.dtype)
        self.start(self.target, self.ref)

    def put_rows(self, start, size, value):
        block = pl.ds(start, size)
        self.ref[block, :] = value.astype(self.ref.dtype)
        self.start(self.target.at[block, :], self.ref.at[block, :])

    def wait(self):
        for copy in self.copies:
            copy.wait()


HBM = pl.BlockSpec(memory_space=pltpu.HBM)
SMEM = pl.BlockSpec(memory_space=pltpu.SMEM)
VMEM = pl.BlockSpec(memory_space=pltpu.VMEM)


class Held:
    def __init__(self, value):
        self.value = value
        self.shape, self.dtype = value.shape, value.dtype


def bare(value):
    return value.value if isinstance(value, Held) else value


def call(body, outs, *args, scalars=0, mib=24, number=False):
    count = len(args)
    held = [k for k in range(scalars, count) if isinstance(args[k], Held)]

    def kernel(*refs):
        sinks = refs[count : count + len(outs)]
        extra = refs[count + len(outs) : count + len(outs) + number]
        scratch = refs[count + len(outs) + number :]
        sink_vmem, held_vmem = scratch[: len(outs)], scratch[len(outs) : len(outs) + len(held)]
        sink_sem, held_sem = scratch[-2], scratch[-1]
        sources = {}
        for k, slot in enumerate(held):
            copy = pltpu.make_async_copy(refs[slot], held_vmem[k], held_sem.at[k])
            copy.start()
            sources[slot] = Source(held_vmem[k], copy)
        results = [
            Sink(sinks[k], sink_vmem[k], sink_sem.at[k])
            for k in range(len(outs))
        ]
        body(*refs[:scalars], *(sources.get(k) or Source(refs[k]) for k in range(scalars, count)), *results, *extra)
        for result in results:
            result.wait()

    specs = [SMEM if k < scalars else HBM if k in held else VMEM for k in range(count)]
    results = pl.pallas_call(
        kernel,
        out_shape=[pltpu.HBM(s, d) for s, d in outs] + [jax.ShapeDtypeStruct((1,), F32)] * number,
        in_specs=specs,
        out_specs=[HBM] * len(outs) + [SMEM] * number,
        scratch_shapes=[pltpu.VMEM(s, d) for s, d in outs]
        + [pltpu.VMEM(args[k].shape, args[k].dtype) for k in held]
        + [pltpu.SemaphoreType.DMA((len(outs), 8)), pltpu.SemaphoreType.DMA((max(1, len(held)),))],
        compiler_params=pltpu.CompilerParams(vmem_limit_bytes=mib * 1024 * 1024),
    )(*(pltpu.with_memory_space_constraint(x.value, pltpu.HBM) if isinstance(x, Held) else x for x in args))
    return [Held(x) for x in results[: len(outs)]] + list(results[len(outs) :])


def pair_scores(blocks, query_parts):
    rows, width = blocks.shape[0], query_parts[0].shape[0]
    parts = split3(blocks)
    wide = mm(jnp.concatenate(parts, axis=0), jnp.concatenate(query_parts[:2], axis=0), 1, 1)
    small = wide[2 * rows :, :width] + wide[rows : 2 * rows, width:] + mm(parts[0], query_parts[2], 1, 1)
    return (wide[:rows, :width] + (wide[:rows, width:] + wide[rows : 2 * rows, :width] + small)) * score_scale


def hard_kernel(base_ref, qa, ia, qb, ib, table, na, nb, made_a, made_b, stat_a, stat_b, stack, first=None):
    a_parts, b_parts = split3(qa.get()), split3(qb.get())
    width = a_parts[0].shape[0]
    stack.put(jnp.concatenate(a_parts[:2] + b_parts[:2], axis=0))
    if first is not None:
        first(a_parts)
    wide = mm(table.get(), jnp.concatenate(a_parts + b_parts, axis=0), 1, 1)
    weights = []
    for slot, (index, named, stat) in enumerate(((ia, na, stat_a), (ib, nb, stat_b))):
        value = table_scores(wide[:, 3 * slot * width : 3 * (slot + 1) * width], index.get(), base_ref[0])
        named.put(value)
        top = jnp.max(value, axis=0, keepdims=True)
        value = jnp.exp(value - top)
        total = jnp.sum(value, axis=0, keepdims=True)
        stat.put(
            jnp.concatenate([jnp.broadcast_to(top, (4, width)), jnp.broadcast_to(total, (4, width))], axis=0)
        )
        weights += split2(value)
    pair = mm(jnp.concatenate(weights, axis=1), table.get(), 0, 0)
    made_a.put(pair[:width] + pair[width : 2 * width])
    made_b.put(pair[2 * width : 3 * width] + pair[3 * width :])


def first_hard_kernel(base_ref, qa, ia, qb, ib, table, passage, na, nb, made_a, made_b, stat_a, stat_b, stack, score):
    def first(parts):
        score.put(pair_scores(passage.get(), parts))

    hard_kernel(base_ref, qa, ia, qb, ib, table, na, nb, made_a, made_b, stat_a, stat_b, stack, first)


def is_eye(rows):
    shape = (rows, rows)
    return lax.broadcasted_iota(jnp.int32, shape, 0) == lax.broadcasted_iota(jnp.int32, shape, 1)


def window_kernel(query, p1, p2, p3, s0, t0, t1, t2, t3, w0, w1, w2, w3, lse, news):
    parts = split3(query.get())
    rows = parts[0].shape[0]
    blocks = jnp.concatenate([p1.get(), p2.get(), p3.get()], axis=0)
    found = pair_scores(blocks, parts)
    scores = [s0.get(), found[:rows], found[rows : 2 * rows], found[2 * rows :]]
    positive = jnp.sum(jnp.where(is_eye(rows), scores[0], 0.0), axis=0, keepdims=True)
    stats = [stat.get() for stat in (t0, t1, t2, t3)]
    top = stats[0][0:1]
    for stat in stats[1:]:
        top = jnp.maximum(top, stat[0:1])
    for score in scores:
        top = jnp.maximum(top, jnp.max(score, axis=0, keepdims=True))
    total = jnp.zeros_like(top)
    for stat in stats:
        total = total + stat[4:5] * jnp.exp(stat[0:1] - top)
    for score in scores:
        total = total + jnp.sum(jnp.exp(score - top), axis=0, keepdims=True)
    result = top + jnp.log(total)
    odd = lax.broadcasted_iota(jnp.int32, news.ref.shape, 0) % 2 == 1
    news.put(jnp.where(odd, result - positive, result))
    lse.put(jnp.broadcast_to(result, (8, rows)))
    for out, score in zip((w1, w2, w3, w0), scores[1:] + scores[:1]):
        out.put(jnp.exp(score - result))


def query_grad_kernel(
    lse, w0, w1, w2, w3, p0, p1, p2, p3, t0, t1, t2, t3, m0, m1, m2, m3, out
):
    row = lse.get()[0:1, :]
    rows = row.shape[1]
    eye = is_eye(rows)
    hi, lo = split2(jnp.concatenate([w.get() for w in (w0, w1, w2, w3)], axis=0))
    block_hi, block_lo = split2(jnp.concatenate([p.get() for p in (p0, p1, p2, p3)], axis=0))
    wide = mm(jnp.concatenate([hi, lo], axis=1), block_hi, 0, 0)
    total = wide[:rows] + (wide[rows:] + mm(hi, block_lo, 0, 0))
    for stat, made in ((t0, m0), (t1, m1), (t2, m2), (t3, m3)):
        ratio = jnp.broadcast_to(jnp.exp(stat.get()[0:1, :] - row), (rows, rows))
        column = jnp.sum(jnp.where(eye, ratio, 0.0), axis=1, keepdims=True)
        total = total + column * made.get().astype(F32)
    out.put(score_scale * (total - p0.get()))


def passage_grad_kernel(q0, q1, q2, q3, w0, w1, w2, w3, out):
    rows = w0.ref.shape[0]
    hi, lo = split2(jnp.concatenate([w.get() for w in (w0, w1, w2, w3)], axis=1))
    own_hi, own_lo = split2(q0.get())
    wide = mm(jnp.concatenate([hi, lo], axis=0), jnp.concatenate([own_hi, q1.get(), q2.get(), q3.get()], axis=0), 1, 0)
    total = wide[:rows] + (wide[rows:] + mm(hi[:, :rows], own_lo, 1, 0))
    out.put(score_scale * total - score_scale * q0.get())


def table_grad_kernel(base_ref, news, n0, n1, n2, n3, s01, s23, out, loss_ref):
    own = base_ref[2]
    rows_here = news.ref[pl.ds(pl.multiple_of(base_ref[1], 8), 8), :]
    lses = []
    for flip in range(4):
        lse = jnp.zeros((1, rows_here.shape[1]), F32)
        for owner in range(4):
            lse = lse + jnp.where((own ^ flip) == owner, rows_here[2 * owner : 2 * owner + 1, :], 0.0)
        lses.append(lse)
    stacks = [s01.get(), s23.get()]
    listed = [n.get() for n in (n0, n1, n2, n3)]
    size = TABLE_BLOCK
    for start in range(0, listed[0].shape[0], size):
        parts = []
        for value, lse in zip(listed, lses):
            weight = jnp.exp(value[start : start + size] - lse).astype(BF16)
            parts += [weight, weight]
        total = mm(jnp.concatenate(parts[:4], axis=1), stacks[0], 1, 0)
        total = total + mm(jnp.concatenate(parts[4:], axis=1), stacks[1], 1, 0)
        out.put_rows(start, size, score_scale * total)
    odd = lax.broadcasted_iota(jnp.int32, news.ref.shape, 0) % 2 == 1
    count = news.ref.shape[0] // 2 * news.ref.shape[1]
    loss_ref[0] = jnp.sum(jnp.where(odd, news.get(), 0.0)) / count


def named(move, value, *args, **kwargs):
    return move(bare(value), *args, **kwargs)


def step(queries, passages, hard_table, hard_index):
    rows, width = queries.shape
    table_rows = hard_table.shape[0]
    device_count = lax.axis_size(BLK) * lax.axis_size(GRP)
    index = hard_index.T
    mine = lax.axis_index(GRP).astype(jnp.int32)
    here = lax.axis_index(BLK).astype(jnp.int32)
    base = jnp.stack([mine * table_rows, here * 8, mine])
    short = queries.astype(BF16)
    queries, passages, hard_table = Held(queries), Held(passages), Held(hard_table)
    listed = ((table_rows, rows), F32)
    tile = ((8, rows), F32)
    full = ((rows, width), F32)
    half = ((rows, width), BF16)
    square = ((rows, rows), F32)
    stacked = ((4 * rows, width), BF16)

    q_far = named(swapped, queries, "grp_0")
    i_far = named(swapped, index, "grp_0")
    p_one = named(along_loop, passages, 1)
    p_two = named(along_loop, passages, 2)
    q_near = named(swapped, queries, "grp_1")
    i_near = named(swapped, index, "grp_1")
    n0, n1, made_0, near_made, stat_0, near_stat, stack_01, s0 = call(
        first_hard_kernel, [listed, listed, full, half, tile, tile, stacked, square],
        base, queries, index, q_near, i_near, hard_table, passages, scalars=1,
    )
    b_two = named(along_loop, short, -2)
    q_diag = named(swapped, q_far, "grp_1")
    i_diag = named(swapped, i_far, "grp_1")
    p_three = named(along_loop, p_one, 2)
    n2, n3, far_made, diag_made, far_stat, diag_stat, stack_23 = call(
        hard_kernel, [listed, listed, half, half, tile, tile, stacked],
        base, q_far, i_far, q_diag, i_diag, hard_table, scalars=1,
    )
    stat_1 = named(swapped, near_stat, "grp_1")
    stat_2 = named(swapped, far_stat, "grp_0")
    stat_3 = named(crossed, diag_stat)
    made_1 = named(swapped, near_made, "grp_1")
    made_2 = named(swapped, far_made, "grp_0")
    made_3 = named(crossed, diag_made)
    b_one = named(along_loop, short, -1)
    b_three = named(along_loop, b_one, -2)

    w0, w1, w2, w3, lse, news = call(
        window_kernel, [square, square, square, square, tile, ((2 * device_count, rows), F32)],
        queries, p_one, p_two, p_three, s0, stat_0, stat_1, stat_2, stat_3,
    )
    all_news = lax.all_to_all(bare(news), BLK_GRP, 0, 0, tiled=True)
    v1 = named(along_loop, w1, -1)
    v2 = named(along_loop, w2, -2)
    v3 = named(along_loop, w3, -3)

    (query_grad,) = call(
        query_grad_kernel, [full],
        lse, w0, w1, w2, w3, passages, p_one, p_two, p_three,
        stat_0, stat_1, stat_2, stat_3, made_0, made_1, made_2, made_3,
    )
    (passage_grad,) = call(
        passage_grad_kernel, [full],
        queries, b_one, b_two, b_three, w0, v1, v2, v3,
    )
    table_grad, mean_loss = call(
        table_grad_kernel, [((table_rows, width), BF16)],
        base, all_news, n0, n1, n2, n3, stack_01, stack_23, scalars=1, number=True,
    )
    return (mean_loss.reshape(()), bare(query_grad), bare(passage_grad), bare(table_grad))


def solution(mesh):
    finer = Mesh(mesh.devices.reshape(4, 4, 2, 2, 2), ("blk_0", "blk_1", "blk_2", "grp_0", "grp_1"))
    in_specs = (P(BLK_GRP, None), P(BLK_GRP, None), P(BLK_GRP, None), P(BLK_GRP, None))
    out_specs = (P(), P(BLK_GRP, None), P(BLK_GRP, None), P(BLK_GRP, None))
    return jax.shard_map(step, mesh=finer, in_specs=in_specs, out_specs=out_specs, check_vma=False)
```

```python
import jax
import jax.numpy as jnp
from jax import lax
from jax.experimental import pallas as pl
from jax.experimental.pallas import tpu as pltpu
from jax.sharding import Mesh
from jax.sharding import PartitionSpec as P


GRP = ("grp_0", "grp_1")
BLK = ("blk_0", "blk_1", "blk_2")
BLK_GRP = ("blk_0", "blk_1", "blk_2", "grp_0", "grp_1")

score_scale = 0.015625
FLOOR = -1.0e30
TABLE_BLOCK = 256
F32 = jnp.float32
BF16 = jnp.bfloat16


def along_loop(value, by):
    length = lax.axis_size(BLK)
    return lax.ppermute(value, BLK, [(i, (i + by) % length) for i in range(length)])


def swapped(value, axis):
    return lax.ppermute(value, axis, [(0, 1), (1, 0)])


def crossed(value):
    return lax.ppermute(value, GRP, [(0, 3), (1, 2), (2, 1), (3, 0)])


def mm(a, b, ca, cb):
    return lax.dot_general(a, b, (((ca,), (cb,)), ((), ())), preferred_element_type=F32)


def split2(x):
    hi = x.astype(BF16)
    return hi, (x - hi.astype(F32)).astype(BF16)


def split3(x):
    hi = x.astype(BF16)
    rest = x - hi.astype(F32)
    mid = rest.astype(BF16)
    return hi, mid, (rest - mid.astype(F32)).astype(BF16)


def table_scores(wide, index_rows, base):
    width = wide.shape[1] // 3
    score = (wide[:, :width] + (wide[:, width : 2 * width] + wide[:, 2 * width :])) * score_scale
    row_id = lax.broadcasted_iota(jnp.int32, score.shape, 0) + base
    count = jnp.zeros(score.shape, F32)
    for k in range(index_rows.shape[0]):
        count = count + jnp.where(index_rows[k : k + 1, :] == row_id, 1.0, 0.0)
    return jnp.where(count > 0.0, score + jnp.log(jnp.maximum(count, 1.0)), FLOOR)


class Source:
    def __init__(self, ref, copy=None):
        self.ref, self.copy = ref, copy

    def get(self):
        if self.copy is not None:
            self.copy.wait()
            self.copy = None
        return self.ref[...]

    @property
    def shape(self):
        return self.ref.shape

    def rows(self, start, size):
        self.get()
        return self.ref[pl.ds(start, size), :]


class Sink:
    def __init__(self, target, ref, sem):
        self.target, self.ref, self.sem, self.copies = target, ref, sem, []

    def start(self, target, ref):
        copy = pltpu.make_async_copy(ref, target, self.sem.at[len(self.copies)])
        copy.start()
        self.copies.append(copy)

    def put(self, value):
        self.ref[...] = value.astype(self.ref.dtype)
        self.start(self.target, self.ref)

    def put_rows(self, start, size, value):
        block = pl.ds(start, size)
        self.ref[block, :] = value.astype(self.ref.dtype)
        self.start(self.target.at[block, :], self.ref.at[block, :])

    def wait(self):
        for copy in self.copies:
            copy.wait()


HBM = pl.BlockSpec(memory_space=pltpu.HBM)
SMEM = pl.BlockSpec(memory_space=pltpu.SMEM)
VMEM = pl.BlockSpec(memory_space=pltpu.VMEM)


class Held:
    def __init__(self, value):
        self.value = value
        self.shape, self.dtype = value.shape, value.dtype


def bare(value):
    return value.value if isinstance(value, Held) else value


def call(body, outs, *args, scalars=0, mib=24, number=False):
    count = len(args)
    held = [k for k in range(scalars, count) if isinstance(args[k], Held)]

    def kernel(*refs):
        sinks = refs[count : count + len(outs)]
        extra = refs[count + len(outs) : count + len(outs) + number]
        scratch = refs[count + len(outs) + number :]
        sink_vmem, held_vmem = scratch[: len(outs)], scratch[len(outs) : len(outs) + len(held)]
        sink_sem, held_sem = scratch[-2], scratch[-1]
        sources = {}
        for k, slot in enumerate(held):
            copy = pltpu.make_async_copy(refs[slot], held_vmem[k], held_sem.at[k])
            copy.start()
            sources[slot] = Source(held_vmem[k], copy)
        results = [
            Sink(sinks[k], sink_vmem[k], sink_sem.at[k])
            for k in range(len(outs))
        ]
        body(*refs[:scalars], *(sources.get(k) or Source(refs[k]) for k in range(scalars, count)), *results, *extra)
        for result in results:
            result.wait()

    specs = [SMEM if k < scalars else HBM if k in held else VMEM for k in range(count)]
    results = pl.pallas_call(
        kernel,
        out_shape=[pltpu.HBM(s, d) for s, d in outs] + [jax.ShapeDtypeStruct((1,), F32)] * number,
        in_specs=specs,
        out_specs=[HBM] * len(outs) + [SMEM] * number,
        scratch_shapes=[pltpu.VMEM(s, d) for s, d in outs]
        + [pltpu.VMEM(args[k].shape, args[k].dtype) for k in held]
        + [pltpu.SemaphoreType.DMA((len(outs), 8)), pltpu.SemaphoreType.DMA((max(1, len(held)),))],
        compiler_params=pltpu.CompilerParams(vmem_limit_bytes=mib * 1024 * 1024),
    )(*(pltpu.with_memory_space_constraint(x.value, pltpu.HBM) if isinstance(x, Held) else x for x in args))
    return [Held(x) for x in results[: len(outs)]] + list(results[len(outs) :])


def pair_scores(blocks, query_parts):
    rows, width = blocks.shape[0], query_parts[0].shape[0]
    parts = split3(blocks)
    wide = mm(jnp.concatenate(parts, axis=0), jnp.concatenate(query_parts[:2], axis=0), 1, 1)
    small = wide[2 * rows :, :width] + wide[rows : 2 * rows, width:] + mm(parts[0], query_parts[2], 1, 1)
    return (wide[:rows, :width] + (wide[:rows, width:] + wide[rows : 2 * rows, :width] + small)) * score_scale


def hard_kernel(base_ref, qa, ia, qb, ib, table, na, nb, made_a, made_b, stat_a, stat_b, stack, first=None):
    a_parts, b_parts = split3(qa.get()), split3(qb.get())
    width = a_parts[0].shape[0]
    stack.put(jnp.concatenate(a_parts[:2] + b_parts[:2], axis=0))
    if first is not None:
        first(a_parts)
    stack_all = jnp.concatenate(a_parts + b_parts, axis=0)
    rows_in = table.get()
    found = ([], [])
    for start in range(0, rows_in.shape[0], TABLE_BLOCK):
        wide = mm(rows_in[start : start + TABLE_BLOCK], stack_all, 1, 1)
        for slot, index in enumerate((ia, ib)):
            part = wide[:, 3 * slot * width : 3 * (slot + 1) * width]
            found[slot].append(table_scores(part, index.get(), base_ref[0] + start))
    weights = []
    for values, named, stat in zip(found, (na, nb), (stat_a, stat_b)):
        value = jnp.concatenate(values, axis=0)
        named.put(value)
        top = jnp.max(value, axis=0, keepdims=True)
        value = jnp.exp(value - top)
        total = jnp.sum(value, axis=0, keepdims=True)
        stat.put(
            jnp.concatenate([jnp.broadcast_to(top, (4, width)), jnp.broadcast_to(total, (4, width))], axis=0)
        )
        weights += split2(value)
    pair = mm(jnp.concatenate(weights, axis=1), table.get(), 0, 0)
    made_a.put(pair[:width] + pair[width : 2 * width])
    made_b.put(pair[2 * width : 3 * width] + pair[3 * width :])


def first_hard_kernel(base_ref, qa, ia, qb, ib, table, passage, na, nb, made_a, made_b, stat_a, stat_b, stack, score):
    def first(parts):
        score.put(pair_scores(passage.get(), parts))

    hard_kernel(base_ref, qa, ia, qb, ib, table, na, nb, made_a, made_b, stat_a, stat_b, stack, first)


def is_eye(rows):
    shape = (rows, rows)
    return lax.broadcasted_iota(jnp.int32, shape, 0) == lax.broadcasted_iota(jnp.int32, shape, 1)


def window_kernel(query, p1, p2, p3, s0, t0, t1, t2, t3, w0, w1, w2, w3, lse, news):
    parts = split3(query.get())
    rows = parts[0].shape[0]
    blocks = jnp.concatenate([p1.get(), p2.get(), p3.get()], axis=0)
    found = pair_scores(blocks, parts)
    scores = [s0.get(), found[:rows], found[rows : 2 * rows], found[2 * rows :]]
    positive = jnp.sum(jnp.where(is_eye(rows), scores[0], 0.0), axis=0, keepdims=True)
    stats = [stat.get() for stat in (t0, t1, t2, t3)]
    top = stats[0][0:1]
    for stat in stats[1:]:
        top = jnp.maximum(top, stat[0:1])
    for score in scores:
        top = jnp.maximum(top, jnp.max(score, axis=0, keepdims=True))
    total = jnp.zeros_like(top)
    for stat in stats:
        total = total + stat[4:5] * jnp.exp(stat[0:1] - top)
    for score in scores:
        total = total + jnp.sum(jnp.exp(score - top), axis=0, keepdims=True)
    result = top + jnp.log(total)
    odd = lax.broadcasted_iota(jnp.int32, news.ref.shape, 0) % 2 == 1
    news.put(jnp.where(odd, result - positive, result))
    lse.put(jnp.broadcast_to(result, (8, rows)))
    for out, score in zip((w1, w2, w3, w0), scores[1:] + scores[:1]):
        out.put(jnp.exp(score - result))


def query_grad_kernel(
    lse, w0, w1, w2, w3, p0, p1, p2, p3, t0, t1, t2, t3, m0, m1, m2, m3, out
):
    row = lse.get()[0:1, :]
    rows = row.shape[1]
    eye = is_eye(rows)
    hi, lo = split2(jnp.concatenate([w.get() for w in (w0, w1, w2, w3)], axis=0))
    block_hi, block_lo = split2(jnp.concatenate([p.get() for p in (p0, p1, p2, p3)], axis=0))
    wide = mm(jnp.concatenate([hi, lo], axis=1), block_hi, 0, 0)
    total = wide[:rows] + (wide[rows:] + mm(hi, block_lo, 0, 0))
    for stat, made in ((t0, m0), (t1, m1), (t2, m2), (t3, m3)):
        ratio = jnp.broadcast_to(jnp.exp(stat.get()[0:1, :] - row), (rows, rows))
        column = jnp.sum(jnp.where(eye, ratio, 0.0), axis=1, keepdims=True)
        total = total + column * made.get().astype(F32)
    out.put(score_scale * (total - p0.get()))


def passage_grad_kernel(q0, q1, q2, q3, w0, w1, w2, w3, out):
    rows = w0.ref.shape[0]
    hi, lo = split2(jnp.concatenate([w.get() for w in (w0, w1, w2, w3)], axis=1))
    own_hi, own_lo = split2(q0.get())
    wide = mm(jnp.concatenate([hi, lo], axis=0), jnp.concatenate([own_hi, q1.get(), q2.get(), q3.get()], axis=0), 1, 0)
    total = wide[:rows] + (wide[rows:] + mm(hi[:, :rows], own_lo, 1, 0))
    out.put(score_scale * total - score_scale * q0.get())


def table_grad_kernel(base_ref, news, n0, n1, s01, n2, n3, s23, out, loss_ref):
    own = base_ref[2]
    rows_here = news.ref[pl.ds(pl.multiple_of(base_ref[1], 8), 8), :]
    lses = []
    for flip in range(4):
        lse = jnp.zeros((1, rows_here.shape[1]), F32)
        for owner in range(4):
            lse = lse + jnp.where((own ^ flip) == owner, rows_here[2 * owner : 2 * owner + 1, :], 0.0)
        lses.append(lse)
    halves = (((n0, lses[0]), (n1, lses[1]), s01), ((n2, lses[2]), (n3, lses[3]), s23))
    for start in range(0, n0.shape[0], TABLE_BLOCK):
        total = None
        for first, second, stack in halves:
            parts = []
            for listed, lse in (first, second):
                weight = jnp.exp(listed.rows(start, TABLE_BLOCK) - lse).astype(BF16)
                parts += [weight, weight]
            piece = mm(jnp.concatenate(parts, axis=1), stack.get(), 1, 0)
            total = piece if total is None else total + piece
        out.put_rows(start, TABLE_BLOCK, score_scale * total)
    odd = lax.broadcasted_iota(jnp.int32, news.ref.shape, 0) % 2 == 1
    count = news.ref.shape[0] // 2 * news.ref.shape[1]
    loss_ref[0] = jnp.sum(jnp.where(odd, news.get(), 0.0)) / count


def named(move, value, *args, **kwargs):
    return move(bare(value), *args, **kwargs)


def step(queries, passages, hard_table, hard_index):
    rows, width = queries.shape
    table_rows = hard_table.shape[0]
    device_count = lax.axis_size(BLK) * lax.axis_size(GRP)
    index = hard_index.T
    mine = lax.axis_index(GRP).astype(jnp.int32)
    here = lax.axis_index(BLK).astype(jnp.int32)
    base = jnp.stack([mine * table_rows, here * 8, mine])
    short = queries.astype(BF16)
    queries, passages, hard_table = Held(queries), Held(passages), Held(hard_table)
    listed = ((table_rows, rows), F32)
    tile = ((8, rows), F32)
    full = ((rows, width), F32)
    half = ((rows, width), BF16)
    square = ((rows, rows), F32)
    stacked = ((4 * rows, width), BF16)

    q_far = named(swapped, queries, "grp_0")
    i_far = named(swapped, index, "grp_0")
    p_one = named(along_loop, passages, 1)
    p_two = named(along_loop, passages, 2)
    q_near = named(swapped, queries, "grp_1")
    i_near = named(swapped, index, "grp_1")
    n0, n1, made_0, near_made, stat_0, near_stat, stack_01, s0 = call(
        first_hard_kernel, [listed, listed, full, half, tile, tile, stacked, square],
        base, queries, index, q_near, i_near, hard_table, passages, scalars=1,
    )
    b_two = named(along_loop, short, -2)
    q_diag = named(swapped, q_far, "grp_1")
    i_diag = named(swapped, i_far, "grp_1")
    p_three = named(along_loop, p_one, 2)
    n2, n3, far_made, diag_made, far_stat, diag_stat, stack_23 = call(
        hard_kernel, [listed, listed, half, half, tile, tile, stacked],
        base, q_far, i_far, q_diag, i_diag, hard_table, scalars=1,
    )
    stat_1 = named(swapped, near_stat, "grp_1")
    stat_2 = named(swapped, far_stat, "grp_0")
    stat_3 = named(crossed, diag_stat)
    made_1 = named(swapped, near_made, "grp_1")
    made_2 = named(swapped, far_made, "grp_0")
    made_3 = named(crossed, diag_made)
    b_one = named(along_loop, short, -1)
    b_three = named(along_loop, b_one, -2)

    w0, w1, w2, w3, lse, news = call(
        window_kernel, [square, square, square, square, tile, ((2 * device_count, rows), F32)],
        queries, p_one, p_two, p_three, s0, stat_0, stat_1, stat_2, stat_3,
    )
    all_news = lax.all_to_all(bare(news), BLK_GRP, 0, 0, tiled=True)
    v1 = named(along_loop, w1, -1)
    v2 = named(along_loop, w2, -2)
    v3 = named(along_loop, w3, -3)

    (query_grad,) = call(
        query_grad_kernel, [full],
        lse, w0, w1, w2, w3, passages, p_one, p_two, p_three,
        stat_0, stat_1, stat_2, stat_3, made_0, made_1, made_2, made_3,
    )
    (passage_grad,) = call(
        passage_grad_kernel, [full],
        queries, b_one, b_two, b_three, w0, v1, v2, v3,
    )
    table_grad, mean_loss = call(
        table_grad_kernel, [((table_rows, width), BF16)],
        base, all_news, n0, n1, stack_01, n2, n3, stack_23, scalars=1, number=True,
    )
    return (mean_loss.reshape(()), bare(query_grad), bare(passage_grad), bare(table_grad))


def solution(mesh):
    finer = Mesh(mesh.devices.reshape(4, 4, 2, 2, 2), ("blk_0", "blk_1", "blk_2", "grp_0", "grp_1"))
    in_specs = (P(BLK_GRP, None), P(BLK_GRP, None), P(BLK_GRP, None), P(BLK_GRP, None))
    out_specs = (P(), P(BLK_GRP, None), P(BLK_GRP, None), P(BLK_GRP, None))
    return jax.shard_map(step, mesh=finer, in_specs=in_specs, out_specs=out_specs, check_vma=False)
```
